32 devices in a mesh: dp: 8 (over y, x, core), exch: 4 (over z).
Axes of the slice: x: 2, y: 2, z: 4, core: 2. Of those that a mesh axis runs over, the one named last changes fastest.
Arguments:
- x_raw: bfloat16 [1024, 2048], P('exch', 'dp'), may hold values from -6 to 6
- bc_raw: bfloat16 [1024, 256], P(('exch', 'dp')), may hold values from -6 to 6
- dt_raw: bfloat16 [32, 1024], P('dp', 'exch'), may hold values from -4 to 4
- cotangent: bfloat16 [1024, 2048], P('exch', 'dp'), may hold values from -6 to 6
- ssm_state: bfloat16 [8, 32, 64, 128], P('exch', 'dp'), may hold values from -0.625 to 0.625
- conv_x_state: bfloat16 [8, 3, 2048], P('exch', None, 'dp'), may hold values from -6 to 6
- conv_bc_state: bfloat16 [8, 3, 256], P('exch'), may hold values from -6 to 6
- owner: int32 [8], P('exch'), may hold values from 0 to 3, as said below
- resp_len: int32 [8], P('exch'), may hold values from 32 to 128, as said below
- conv_x_weight: float32 [4, 2048], P(None, 'dp'), may hold values from -3 to 3
- conv_bc_weight: float32 [4, 256], replicated, may hold values from -3 to 3
- dt_bias: float32 [32], P('dp'), may hold values from -5 to -3
- a_log: float32 [32], P('dp'), may hold values from -2.3 to 2.1
- skip_d: float32 [32], P('dp'), may hold values from 0.5 to 1.5
Outputs:
- grad_x: bfloat16 [1024, 2048], P('exch', 'dp')
- grad_bc: bfloat16 [1024, 256], P(('exch', 'dp'))
- grad_dt: bfloat16 [32, 1024], P('dp', 'exch')
- grad_conv_x: float32 [4, 2048], P(None, 'dp')
- grad_conv_bc: float32 [4, 256], replicated
- grad_heads: float32 [3, 32], P(None, 'dp')
The draws below stay inside these ranges and needn't reach their ends.
Inputs may be any that keep to these rules, and one draw needn't show every extreme that they name: `owner`: among the 2 prompts of one holder (an aligned block along exch) no learner index occurs more than 1 times, and some learner index occurs exactly 1 times; over all 8 prompts every learner index occurs exactly 2 times. `resp_len`: every learner's block of 2 responses holds a response of length 128.
All inputs are finite; a program needn't handle non-finite values.
Results may differ from the reference program's by a relative error of at most 0.001.
Values may be sent and summed in bfloat16 or wider, within the bound.
A program may use at most 64 MiB of HBM per device.

```python
import jax
import jax.numpy as jnp
from jax import lax

HDIM = 64
NSTATE = 128
KCONV = 4
HEADS_GROUP = 32
SPAN = 128
GROUP = 1
CAP = 1
L = 128
P_DEV = 2
PROMPTS = 8
RESP_DEV = 2
RESPONSES = 8
TOK_DEV = 256
TOKENS = 1024
HEADS = 32
NGROUPS = 1
N_EXCH = 4


def draw_owner(key, part):
    holders = PROMPTS // P_DEV
    order = jax.random.permutation(jax.random.fold_in(key, 11), holders)
    entry = jnp.arange(P_DEV)
    which = jnp.where(entry < CAP, 0, entry - CAP + 1)
    shifts = order[which]
    base = jax.random.fold_in(key, 12)
    holder_keys = jax.vmap(lambda holder: jax.random.fold_in(base, holder))(jnp.arange(holders))
    shuffles = jax.vmap(lambda sub: jax.random.permutation(sub, P_DEV))(holder_keys)
    owners = (jnp.arange(holders)[:, None] + shifts[shuffles]) % holders
    return owners.reshape(-1).astype(jnp.int32)


def draw_resp_len(key, part):
    lengths = jax.random.randint(jax.random.fold_in(key, 21), (RESPONSES,), L // 4, L + 1)
    blocks = RESPONSES // RESP_DEV
    chosen = jax.random.randint(jax.random.fold_in(key, 22), (blocks,), 0, RESP_DEV)
    longest = (jnp.arange(RESP_DEV)[None, :] == chosen[:, None]).reshape(-1)
    return jnp.where(longest, L, lengths).astype(jnp.int32)


def block_levels(stream_key, extent, split, low, largest):
    loudness = 1.0
    for position, shards_of in split:
        steps = jax.random.uniform(jax.random.fold_in(jax.random.fold_in(stream_key, 6), position), (shards_of,), jnp.float32, low / len(split), largest / len(split))
        loudness = loudness * jnp.repeat(jnp.exp(steps), extent[position] // shards_of).reshape((-1,) + (1,) * (len(extent) - 1 - position))
    return loudness


def centred(rng, dims, scale, most, shards=(), kind=jnp.bfloat16):
    entries = jax.random.normal(rng, dims, jnp.float32) * scale
    if len(shards) > 0:
        entries = block_levels(rng, dims, shards, -0.22, 0.18) * entries
    return jnp.clip(entries, min=-most, max=most).astype(kind)


def setup_inputs(seed: int = 0) -> dict:
    seeds = jax.random.split(jax.random.key(seed), 15)
    x_raw = centred(seeds[0], (TOKENS, HEADS * HDIM), 1.0, 6.0, ((0, 4), (1, 8)))
    bc_raw = centred(seeds[1], (TOKENS, NGROUPS * 2 * NSTATE), 1.0, 6.0, ((0, 32),))
    dt_raw = centred(seeds[2], (HEADS, TOKENS), 1.0, 4.0, ((0, 8), (1, 4)))
    cotangent = centred(seeds[3], (TOKENS, HEADS * HDIM), 1.0, 6.0, ((0, 4), (1, 8)))
    ssm_state = centred(seeds[4], (PROMPTS, HEADS, HDIM, NSTATE), 0.1, 0.625, ((0, 4), (1, 8)))
    conv_x_state = centred(seeds[5], (PROMPTS, KCONV - 1, HEADS * HDIM), 1.0, 6.0, ((0, 4), (2, 8)))
    conv_bc_state = centred(seeds[6], (PROMPTS, KCONV - 1, NGROUPS * 2 * NSTATE), 1.0, 6.0, ((0, 4),))
    owner = draw_owner(jax.random.fold_in(seeds[14], 71), 0)
    resp_len = draw_resp_len(jax.random.fold_in(seeds[14], 71), 0)
    conv_x_weight = centred(seeds[9], (KCONV, HEADS * HDIM), KCONV ** -0.5, 3.0, ((1, 8),), jnp.float32)
    conv_bc_weight = centred(seeds[10], (KCONV, NGROUPS * 2 * NSTATE), KCONV ** -0.5, 3.0, (), jnp.float32)
    dt_bias = jnp.clip(-5.0 + 2.0 * jax.random.uniform(seeds[11], (HEADS,), jnp.float32) ** block_levels(seeds[11], (HEADS,), ((0, 8),), -0.2, 0.2), -5.0, -3.0)
    a_log = jnp.clip(-2.3 + 4.3999998569488525 * jax.random.uniform(seeds[12], (HEADS,), jnp.float32) ** block_levels(seeds[12], (HEADS,), ((0, 8),), -0.2, 0.2), -2.3, 2.1)
    skip_d = jnp.clip(0.5 + 1.0 * jax.random.uniform(seeds[13], (HEADS,), jnp.float32) ** block_levels(seeds[13], (HEADS,), ((0, 8),), -0.2, 0.2), 0.5, 1.5)
    return {"x_raw": x_raw, "bc_raw": bc_raw, "dt_raw": dt_raw, "cotangent": cotangent, "ssm_state": ssm_state, "conv_x_state": conv_x_state, "conv_bc_state": conv_bc_state, "owner": owner, "resp_len": resp_len, "conv_x_weight": conv_x_weight, "conv_bc_weight": conv_bc_weight, "dt_bias": dt_bias, "a_log": a_log, "skip_d": skip_d}


PRECISE = lax.Precision.HIGHEST

def conv_pre(raw, state, weight):
    padded = jnp.concatenate([state, raw], axis=1)
    length = raw.shape[1]
    total = padded[:, 0:length] * weight[0]
    for offset in range(1, weight.shape[0]):
        total = total + padded[:, offset:offset + length] * weight[offset]
    return total

def ssd_output(values, proj_b, proj_c, steps, rate, skip, start, block):
    rows, length, heads, width = values.shape
    count = length // block
    value_blocks = values.reshape(rows, count, block, heads, width)
    b_blocks = proj_b.reshape(rows, count, block, proj_b.shape[-1])
    c_blocks = proj_c.reshape(rows, count, block, proj_c.shape[-1])
    step_blocks = steps.reshape(rows, count, block, heads)
    logs = jnp.cumsum(-rate * step_blocks, axis=2)
    causal = jnp.tril(jnp.ones((block, block), jnp.float32))
    spread = logs[:, :, :, None, :] - logs[:, :, None, :, :]
    decays = jnp.exp(jnp.where(causal[:, :, None] > 0.5, spread, 0.0)) * causal[:, :, None]
    scores = jnp.einsum('rntk,rnsk->rnts', c_blocks, b_blocks, precision=PRECISE)
    weighted = value_blocks * step_blocks[..., None]
    mixing = scores[..., None] * decays
    intra = jnp.einsum('rntsh,rnshp->rnthp', mixing, weighted, precision=PRECISE)
    tails = jnp.exp(logs[:, :, -1:, :] - logs)
    gains = jnp.einsum('rnshp,rnsk->rnhpk', weighted * tails[..., None], b_blocks, precision=PRECISE)
    state = start
    pieces = []
    for index in range(count):
        entry = jnp.exp(logs[:, index])
        carried = jnp.einsum('rtk,rhpk->rthp', c_blocks[:, index], state, precision=PRECISE)
        pieces.append(carried * entry[..., None])
        if index + 1 < count:
            state = state * jnp.exp(logs[:, index, -1])[:, :, None, None] + gains[:, index]
    inter = jnp.stack(pieces, axis=1)
    output = intra + inter + skip[:, None] * value_blocks
    return output.reshape(rows, length, heads, width)

def window_loss(x_rows, bc_act, dt_rows, x_weight, bias, decay_log, skip, x_prev, start, cotan, mask, heads, block):
    x_act = jax.nn.silu(conv_pre(x_rows, x_prev, x_weight))
    rows, length, channels = x_rows.shape
    values = x_act.reshape(rows, length, heads, channels // heads)
    half = bc_act.shape[-1] // 2
    steps = jax.nn.softplus(dt_rows + bias)
    output = ssd_output(values, bc_act[..., :half], bc_act[..., half:], steps, jnp.exp(decay_log), skip, start, block)
    return jnp.sum(output.reshape(rows, length, channels) * cotan * mask[..., None])

def reference(x_raw, bc_raw, dt_raw, cotangent, ssm_state, conv_x_state, conv_bc_state, owner, resp_len, conv_x_weight, conv_bc_weight, dt_bias, a_log, skip_d):
    order = jnp.argsort(owner, stable=True).astype(jnp.int32).reshape(N_EXCH, P_DEV)
    group_width = HEADS_GROUP * HDIM
    pair_width = 2 * NSTATE

    def per_slice(flat):
        learner = flat // NGROUPS
        my_group = flat % NGROUPS
        take = jnp.repeat(order[learner], GROUP)
        first = learner * TOK_DEV
        head_first = my_group * HEADS_GROUP
        col_first = my_group * group_width
        bc_first = my_group * pair_width
        x_rows = lax.dynamic_slice(x_raw, (first, col_first), (TOK_DEV, group_width)).astype(jnp.float32).reshape(RESP_DEV, L, group_width)
        bc_rows = lax.dynamic_slice(bc_raw, (first, bc_first), (TOK_DEV, pair_width)).astype(jnp.float32).reshape(RESP_DEV, L, pair_width)
        cot_rows = lax.dynamic_slice(cotangent, (first, col_first), (TOK_DEV, group_width)).astype(jnp.float32).reshape(RESP_DEV, L, group_width)
        dt_rows = lax.dynamic_slice(dt_raw, (head_first, first), (HEADS_GROUP, TOK_DEV)).astype(jnp.float32).T.reshape(RESP_DEV, L, HEADS_GROUP)
        lengths = lax.dynamic_slice_in_dim(resp_len, learner * RESP_DEV, RESP_DEV, 0)
        live_mask = (jnp.arange(L, dtype=jnp.int32)[None, :] < lengths[:, None]).astype(jnp.float32)
        start_state = lax.dynamic_slice_in_dim(ssm_state, head_first, HEADS_GROUP, 1)[take].astype(jnp.float32)
        x_prev = lax.dynamic_slice_in_dim(conv_x_state, col_first, group_width, 2)[take].astype(jnp.float32)
        bc_prev = lax.dynamic_slice_in_dim(conv_bc_state, bc_first, pair_width, 2)[take].astype(jnp.float32)
        x_weight = lax.dynamic_slice_in_dim(conv_x_weight, col_first, group_width, 1)
        bc_weight = lax.dynamic_slice_in_dim(conv_bc_weight, bc_first, pair_width, 1)
        bias_part = lax.dynamic_slice_in_dim(dt_bias, head_first, HEADS_GROUP, 0)
        decay_part = lax.dynamic_slice_in_dim(a_log, head_first, HEADS_GROUP, 0)
        skip_part = lax.dynamic_slice_in_dim(skip_d, head_first, HEADS_GROUP, 0)

        def total(x_in, bc_in, dt_in, xw_in, bcw_in, bias, decay_log, skip):
            bc_act = jax.nn.silu(conv_pre(bc_in, bc_prev, bcw_in))
            return window_loss(x_in, bc_act, dt_in, xw_in, bias, decay_log, skip, x_prev, start_state, cot_rows, live_mask, HEADS_GROUP, SPAN)
        return jax.grad(total, argnums=(0, 1, 2, 3, 4, 5, 6, 7))(x_rows, bc_rows, dt_rows, x_weight, bc_weight, bias_part, decay_part, skip_part)
    grad_xr, grad_bcr, grad_dtr, grad_wx, grad_wbc, grad_bias, grad_decay, grad_skip = lax.map(per_slice, jnp.arange(N_EXCH * NGROUPS, dtype=jnp.int32))
    grad_x = grad_xr.reshape(N_EXCH, NGROUPS, TOK_DEV, group_width).transpose(0, 2, 1, 3).reshape(TOKENS, HEADS * HDIM).astype(jnp.bfloat16)
    grad_bc = grad_bcr.reshape(N_EXCH, NGROUPS, TOK_DEV, pair_width).transpose(0, 2, 1, 3).reshape(TOKENS, NGROUPS * pair_width).astype(jnp.bfloat16)
    grad_dt = grad_dtr.reshape(N_EXCH, NGROUPS, TOK_DEV, HEADS_GROUP).transpose(1, 3, 0, 2).reshape(HEADS, TOKENS).astype(jnp.bfloat16)
    grad_conv_x = lax.optimization_barrier(jnp.sum(grad_wx.reshape(N_EXCH, NGROUPS, KCONV, group_width), axis=0)).transpose(1, 0, 2).reshape(KCONV, HEADS * HDIM)
    grad_conv_bc = lax.optimization_barrier(jnp.sum(grad_wbc.reshape(N_EXCH, NGROUPS, KCONV, pair_width), axis=0)).transpose(1, 0, 2).reshape(KCONV, NGROUPS * pair_width)
    grad_heads = jnp.stack([lax.optimization_barrier(jnp.sum(grad_bias.reshape(N_EXCH, HEADS), axis=0)), lax.optimization_barrier(jnp.sum(grad_decay.reshape(N_EXCH, HEADS), axis=0)), lax.optimization_barrier(jnp.sum(grad_skip.reshape(N_EXCH, HEADS), axis=0))])
    return (grad_x, grad_bc, grad_dt, grad_conv_x, grad_conv_bc, grad_heads)
```

```python
import functools

import jax
import jax.numpy as jnp
from jax import lax
from jax.experimental import pallas as pl
from jax.experimental.pallas import tpu as pltpu
from jax.sharding import PartitionSpec as P

DEV_GROUP = 8
GROUP = 1
MESH = pl.DeviceIdType.MESH
F32 = jnp.float32
BF16 = jnp.bfloat16


def nn(a, b):
    return lax.dot_general(a, b, (((1,), (0,)), ((), ())), preferred_element_type=F32)


def nt(a, b):
    return lax.dot_general(a, b, (((1,), (1,)), ((), ())), preferred_element_type=F32)


def split(a):
    high = a.astype(BF16)
    return high, (a - high.astype(F32)).astype(BF16)


def three(dot, a, b):
    return dot(a[0], b[0]) + (dot(a[0], b[1]) + dot(a[1], b[0]))


def iota(shape, dim):
    return lax.broadcasted_iota(jnp.int32, shape, dim)


def kernel(
    peers, slices, groups, owner, lens, bias, a_log, skip, x_ref, bc_ref, dt_ref, cot_ref,
    ssm_ref, cx_ref, cbc_ref, wx_ref, wbc_ref,
    gx_ref, gbc_ref, gdt_ref, gwx_ref, gtaps_ref, gheads_ref,
    msg, state, gath, msg_out, state_out, pad_x, pad_bc, dpx, dpbc, dw_ref, taps, raw, back,
    fin, sem_msg, sem_state, sem_gath, sem_taps, sem_back, sem_fin,
):
    mine = lax.axis_index("exch")
    me = lax.axis_index("dp")
    prompts, depth, channels = cx_ref.shape
    taps_n = depth + 1
    responses = lens.shape[0]
    heads = bias.shape[0]
    width = channels // heads
    tokens = x_ref.shape[0]
    length = tokens // responses
    rows = bc_ref.shape[0]
    pair = cbc_ref.shape[2]
    half = pair // 2
    lanes = responses * heads
    base = 8 - depth

    def along(offset):
        return {"exch": lax.rem(mine + offset, peers)}

    def across(offset):
        return {"dp": lax.rem(me + offset, slices)}

    barrier = pltpu.get_barrier_semaphore()
    for offset in range(1, slices):
        pl.semaphore_signal(barrier, inc=1, device_id=across(offset), device_id_type=MESH)
    for offset in range(1, peers):
        pl.semaphore_signal(barrier, inc=1, device_id=along(offset), device_id_type=MESH)

    def fill(target, msg_dst, state_dst):
        small = jnp.zeros((depth, channels + pair), F32)
        flag = jnp.zeros((1, channels + pair), F32)
        big = jnp.zeros(ssm_ref.shape[1:], F32)
        for p in range(prompts):
            weight = (owner[p] == target).astype(F32)
            both = jnp.concatenate([cx_ref[p].astype(F32), cbc_ref[p].astype(F32)], axis=1)
            small = small + both * weight
            flag = flag + weight
            big = big + ssm_ref[p].astype(F32) * weight
        msg_dst[0:depth] = small
        msg_dst[depth : depth + 1] = flag
        state_dst[...] = big.astype(BF16)

    for offset in range(1, peers):
        fill(lax.rem(mine + offset, peers), msg_out.at[offset], state_out.at[offset])
    fill(mine, msg.at[mine], state.at[mine])

    pl.semaphore_wait(barrier, slices - 1 + peers - 1)

    def remote(src, dst, sem, offset, where):
        copy = pltpu.make_async_remote_copy(
            src_ref=src,
            dst_ref=dst,
            send_sem=sem.at[0, offset],
            recv_sem=sem.at[1, offset],
            device_id=where,
            device_id_type=MESH,
        )
        copy.start()
        return copy

    def group_columns(ref, who):
        if groups == 1:
            return ref
        start = pl.multiple_of((who // DEV_GROUP) * pair, pair)
        return ref.at[:, pl.ds(start, pair)]

    msg_copies = [
        remote(msg_out.at[o], msg.at[mine], sem_msg, o, along(o)) for o in range(1, peers)
    ]
    gath_copies = [
        remote(
            group_columns(bc_ref, lax.rem(me + o, slices)),
            gath.at[me],
            sem_gath,
            o,
            across(o),
        )
        for o in range(1, slices)
    ]
    state_copies = [
        remote(state_out.at[o], state.at[mine], sem_state, o, along(o))
        for o in range(peers - 1, 0, -1)
    ]
    gath[me] = group_columns(bc_ref, me)[...]

    row_head = lax.rem(iota((lanes, 1), 0), heads)

    def per_row(ref):
        out = jnp.zeros((lanes, 1), F32)
        for h in range(heads):
            out = jnp.where(row_head == h, ref[h], out)
        return out

    lane_head = iota((1, channels), 1) // width
    skip_row = jnp.zeros((1, channels), F32)
    for h in range(heads):
        skip_row = jnp.where(lane_head == h, skip[h], skip_row)
    dt_in = jnp.concatenate(
        [dt_ref[:, r * length : (r + 1) * length].astype(F32) for r in range(responses)], axis=0
    )
    dt_pre = dt_in + per_row(bias)
    small = jnp.exp(-jnp.abs(dt_pre))
    above = 1.0 + small
    log1p = jnp.where(above == 1.0, small, jnp.log(above) * (small / (above - 1.0)))
    dt = jnp.maximum(dt_pre, 0.0) + log1p
    rate = jnp.exp(per_row(a_log))
    first = iota((length, length), 0)
    second = iota((length, length), 1)
    upto = (first <= second).astype(F32)
    onward = (first >= second).astype(F32)
    causal = first <= second
    logs = lax.dot_general(
        -rate * dt,
        upto,
        (((1,), (0,)), ((), ())),
        preferred_element_type=F32,
        precision=lax.Precision.HIGHEST,
    )
    entry = jnp.exp(logs)
    logs_col = logs.T
    dt_col = dt.T
    entry_col = entry.T

    def spread_heads(cols, r):
        parts = [
            jnp.broadcast_to(cols[:, r * heads + h : r * heads + h + 1], (length, width))
            for h in range(heads)
        ]
        return jnp.concatenate(parts, axis=1)

    def indicator(r):
        row = iota((lanes, channels), 0)
        head = iota((lanes, channels), 1) // width
        return (row == r * heads + head).astype(BF16)

    for r in range(responses):
        block = slice(r * length, (r + 1) * length)
        pad_x[r, 8 : 8 + length] = x_ref[block].astype(F32)
    cots = []
    for r in range(responses):
        block = slice(r * length, (r + 1) * length)
        live = iota((length, 1), 0) < lens[r]
        cots.append(jnp.where(live, cot_ref[block].astype(F32), 0.0))

    for copy in msg_copies:
        copy.wait_recv()
    weights = [[None] * peers for _ in range(prompts)]
    seen = jnp.zeros((1, channels + pair), F32)
    for z in range(peers):
        present = msg[z, depth : depth + 1]
        for j in range(prompts):
            weights[j][z] = jnp.where(seen == float(j), present, 0.0)
        seen = seen + present
    for r in range(responses):
        prev = jnp.zeros((depth, channels + pair), F32)
        for z in range(peers):
            prev = prev + msg[z, 0:depth] * weights[r // GROUP][z]
        pad_x[r, base:8] = prev[:, :channels]
        pad_bc[r, base:8] = prev[:, channels:]

    def convolve(pad, weight, r):
        pre = pad[r, base : base + length] * weight[0:1]
        for k in range(1, taps_n):
            pre = pre + pad[r, base + k : base + k + length] * weight[k : k + 1]
        gate = 1.0 / (1.0 + jnp.exp(-pre))
        return pre * gate, gate * (1.0 + pre * (1.0 - gate))

    wx = wx_ref[...]
    wbc = wbc_ref[...]
    x_acts = [convolve(pad_x, wx, r) for r in range(responses)]

    for copy in gath_copies:
        copy.wait_recv()
    slots = length // rows
    for d in range(slices):
        r, place = d // slots, d % slots
        pad_bc[r, 8 + place * rows : 8 + (place + 1) * rows] = gath[d].astype(F32)
    bc_acts = [convolve(pad_bc, wbc, r) for r in range(responses)]

    across_rows = jnp.zeros((lanes, length), F32)
    dt_first = jnp.zeros((lanes, length), F32)
    row_index = iota((lanes, 1), 0)
    skip_sum = jnp.zeros((1, channels), F32)
    grad_wx = jnp.zeros((taps_n, channels), F32)
    b_grads, c_grads = [], []

    def weight_grad(grad, pad, r):
        parts = [
            jnp.sum(grad * pad[r, base + k : base + k + length], axis=0, keepdims=True)
            for k in range(taps_n)
        ]
        return jnp.concatenate(parts, axis=0)

    def input_grad(ref, weight, r):
        total = ref[r, depth : depth + length] * weight[0:1]
        for k in range(1, taps_n):
            total = total + ref[r, depth - k : depth - k + length] * weight[k : k + 1]
        return total

    for r in range(responses):
        act, slope = x_acts[r]
        cot = cots[r]
        cot_b = cot.astype(BF16)
        dt_full = spread_heads(dt_col, r)
        weighted = split(act * dt_full)
        proj_b = split(bc_acts[r][0][:, :half])
        proj_c = split(bc_acts[r][0][:, half:])
        scores = three(nt, proj_b, proj_c)
        score_grad = jnp.zeros((length, length), F32)
        for h in range(heads):
            i = r * heads + h
            cols = slice(h * width, (h + 1) * width)
            cot_h = cot_b[:, cols]
            gap = logs[i : i + 1] - logs_col[:, i : i + 1]
            decay = jnp.where(causal, jnp.exp(jnp.where(causal, gap, 0.0)), 0.0)
            mix = scores * decay
            mix_grad = nt(weighted[0][:, cols], cot_h) + nt(weighted[1][:, cols], cot_h)
            high, low = split(mix)
            dw_ref[r, :, cols] = nn(high, cot_h) + nn(low, cot_h)
            score_grad = score_grad + mix_grad * decay
            found = jnp.sum(mix_grad * mix, axis=0, keepdims=True)
            across_rows = jnp.where(row_index == i, found, across_rows)
        dw = dw_ref[r]
        prod = split(dw * act)
        mark = indicator(r)
        dt_first = dt_first + (nt(mark, prod[0]) + nt(mark, prod[1]))
        skip_sum = skip_sum + jnp.sum(cot * act, axis=0, keepdims=True)
        pre_grad = (dw * dt_full + skip_row * cot) * slope
        dpx[r, 0:length] = pre_grad
        dpx[r, length : length + 8] = jnp.zeros((8, channels), F32)
        grad_wx = grad_wx + weight_grad(pre_grad, pad_x, r)
        gx_ref[r * length : (r + 1) * length] = input_grad(dpx, wx, r).astype(BF16)
        b_grads.append(three(nn, split(score_grad), proj_c))
        c_grads.append(three(nn, split(score_grad.T), proj_b))

    for copy in state_copies:
        copy.wait_recv()
    starts = []
    grad_taps = jnp.zeros((taps_n, pair), F32)
    for r in range(responses):
        start = jnp.zeros(state.shape[1:], F32)
        for z in range(peers):
            pick = weights[r // GROUP][z][:, : state.shape[2]]
            start = start + state[z].astype(F32) * pick
        start = start.astype(BF16)
        starts.append(start)
        fed = split(cots[r] * spread_heads(entry_col, r))
        c_grad = c_grads[r] + (nn(fed[0], start) + nn(fed[1], start))
        slope = bc_acts[r][1]
        pre_grad = jnp.concatenate([b_grads[r], c_grad], axis=1) * slope
        dpbc[r, 0:length] = pre_grad
        dpbc[r, length : length + 8] = jnp.zeros((8, pair), F32)
        grad_taps = grad_taps + weight_grad(pre_grad, pad_bc, r)

    taps[me, 0:taps_n] = grad_taps
    taps_copies = [
        remote(taps.at[me], taps.at[me], sem_taps, o, across(o)) for o in range(1, slices)
    ]
    for r in range(responses):
        block = input_grad(dpbc, wbc, r)
        for place in range(slots):
            raw[r * slots + place] = block[place * rows : (place + 1) * rows]
    back_copies = [
        remote(raw.at[lax.rem(me + o, slices)], back.at[me], sem_back, o, across(o))
        for o in range(1, slices)
    ]
    back[me] = raw[me]

    entry_grad = jnp.zeros((lanes, length), F32)
    for r in range(responses):
        proj_c = split(bc_acts[r][0][:, half:])
        carried = nt(proj_c[0], starts[r]) + nt(proj_c[1], starts[r])
        prod = split(carried * cots[r])
        mark = indicator(r)
        entry_grad = entry_grad + (nt(mark, prod[0]) + nt(mark, prod[1]))
    log_grad = across_rows + entry * entry_grad - dt * dt_first
    step_grad = lax.dot_general(
        log_grad,
        onward,
        (((1,), (0,)), ((), ())),
        preferred_element_type=F32,
        precision=lax.Precision.HIGHEST,
    )
    dt_grad = dt_first - rate * step_grad
    raw_grad = dt_grad * (1.0 / (1.0 + jnp.exp(-dt_pre)))
    for r in range(responses):
        gdt_ref[:, r * length : (r + 1) * length] = raw_grad[
            r * heads : (r + 1) * heads
        ].astype(BF16)
    bias_rows = jnp.sum(raw_grad, axis=1, keepdims=True)
    decay_rows = -rate * jnp.sum(dt * step_grad, axis=1, keepdims=True)
    bias_grad = jnp.zeros((heads, 1), F32)
    decay_grad = jnp.zeros((heads, 1), F32)
    for r in range(responses):
        bias_grad = bias_grad + bias_rows[r * heads : (r + 1) * heads]
        decay_grad = decay_grad + decay_rows[r * heads : (r + 1) * heads]
    own = iota((heads, channels), 0) == iota((heads, channels), 1) // width
    skip_grad = jnp.sum(jnp.where(own, skip_sum, 0.0), axis=1, keepdims=True)
    column = iota((heads, half), 1)
    head_block = jnp.where(
        column == 0,
        bias_grad,
        jnp.where(column == 1, decay_grad, jnp.where(column == 2, skip_grad, 0.0)),
    )
    fin[mine, 0:taps_n, 0:channels] = grad_wx
    fin[mine, 8 : 8 + heads, 0:half] = head_block

    for copy in taps_copies:
        copy.wait_recv()
    for q in range(groups):
        total = taps[q * DEV_GROUP, 0:taps_n]
        for d in range(1, DEV_GROUP):
            total = total + taps[q * DEV_GROUP + d, 0:taps_n]
        fin[mine, 16 : 16 + taps_n, q * pair : (q + 1) * pair] = total
    fin_copies = [
        remote(fin.at[mine], fin.at[mine], sem_fin, o, along(o)) for o in range(1, peers)
    ]

    for copy in back_copies:
        copy.wait_recv()
    for q in range(groups):
        total = back[q * DEV_GROUP]
        for d in range(1, DEV_GROUP):
            total = total + back[q * DEV_GROUP + d]
        gbc_ref[:, q * pair : (q + 1) * pair] = total.astype(BF16)

    for copy in fin_copies:
        copy.wait_recv()
    wx_total = fin[0, 0:taps_n, 0:channels]
    head_total = fin[0, 8:16, 0:half]
    taps_total = fin[0, 16 : 16 + taps_n, 0 : groups * pair]
    for z in range(1, peers):
        wx_total = wx_total + fin[z, 0:taps_n, 0:channels]
        head_total = head_total + fin[z, 8:16, 0:half]
        taps_total = taps_total + fin[z, 16 : 16 + taps_n, 0 : groups * pair]
    gwx_ref[...] = wx_total
    gtaps_ref[...] = taps_total
    gheads_ref[...] = head_total.T[0:3, 0:heads]
    for copy in msg_copies + gath_copies + state_copies + taps_copies + back_copies + fin_copies:
        copy.wait_send()


def local(
    x_raw, bc_raw, dt_raw, cotangent, ssm_state, conv_x_state, conv_bc_state, owner, resp_len,
    conv_x_weight, conv_bc_weight, dt_bias, a_log, skip_d,
):
    peers = lax.axis_size("exch")
    slices = lax.axis_size("dp")
    prompts, heads, width, nstate = ssm_state.shape
    channels = x_raw.shape[1]
    pair = 2 * nstate
    depth = conv_x_state.shape[1]
    responses = resp_len.shape[0]
    tokens = x_raw.shape[0]
    length = tokens // responses
    rows, all_pairs = bc_raw.shape
    groups = all_pairs // pair
    bc_state, bc_weight = conv_bc_state, conv_bc_weight
    if groups > 1:
        first = (lax.axis_index("dp") // DEV_GROUP) * pair
        bc_state = lax.dynamic_slice_in_dim(conv_bc_state, first, pair, 2)
        bc_weight = lax.dynamic_slice_in_dim(conv_bc_weight, first, pair, 1)
    ssm = ssm_state.reshape(prompts, heads * width, nstate)
    wide = max(all_pairs, channels)
    vmem = pl.BlockSpec(memory_space=pltpu.VMEM)
    smem = pl.BlockSpec(memory_space=pltpu.SMEM)
    dma = pltpu.SemaphoreType.DMA
    outs = (
        jax.ShapeDtypeStruct((tokens, channels), BF16),
        jax.ShapeDtypeStruct((rows, all_pairs), BF16),
        jax.ShapeDtypeStruct((heads, tokens), BF16),
        jax.ShapeDtypeStruct((depth + 1, channels), F32),
        jax.ShapeDtypeStruct((depth + 1, all_pairs), F32),
        jax.ShapeDtypeStruct((3, heads), F32),
    )
    return pl.pallas_call(
        functools.partial(kernel, peers, slices, groups),
        out_shape=outs,
        in_specs=[smem] * 5 + [vmem] * 9,
        out_specs=[vmem] * 6,
        scratch_shapes=[
            pltpu.VMEM((peers, 8, channels + pair), F32),
            pltpu.VMEM((peers, heads * width, nstate), BF16),
            pltpu.VMEM((slices, rows, pair), BF16),
            pltpu.VMEM((peers, 8, channels + pair), F32),
            pltpu.VMEM((peers, heads * width, nstate), BF16),
            pltpu.VMEM((responses, length + 8, channels), F32),
            pltpu.VMEM((responses, length + 8, pair), F32),
            pltpu.VMEM((responses, length + 8, channels), F32),
            pltpu.VMEM((responses, length + 8, pair), F32),
            pltpu.VMEM((responses, length, channels), F32),
            pltpu.VMEM((slices, 8, pair), F32),
            pltpu.VMEM((slices, rows, pair), F32),
            pltpu.VMEM((slices, rows, pair), F32),
            pltpu.VMEM((peers, 24, wide), F32),
            dma((2, peers)),
            dma((2, peers)),
            dma((2, slices)),
            dma((2, slices)),
            dma((2, slices)),
            dma((2, peers)),
        ],
        compiler_params=pltpu.CompilerParams(collective_id=0, has_side_effects=True),
    )(
        owner, resp_len, dt_bias, a_log, skip_d, x_raw, bc_raw, dt_raw, cotangent, ssm,
        conv_x_state, bc_state, conv_x_weight, bc_weight,
    )


def solution(mesh):
    in_specs = (
        P("exch", "dp"),
        P(("exch", "dp"), None),
        P("dp", "exch"),
        P("exch", "dp"),
        P("exch", "dp", None, None),
        P("exch", None, "dp"),
        P("exch", None, None),
        P("exch"),
        P("exch"),
        P(None, "dp"),
        P(),
        P("dp"),
        P("dp"),
        P("dp"),
    )
    out_specs = (
        P("exch", "dp"),
        P(("exch", "dp"), None),
        P("dp", "exch"),
        P(None, "dp"),
        P(),
        P(None, "dp"),
    )
    return jax.shard_map(local, mesh=mesh, in_specs=in_specs, out_specs=out_specs, check_vma=False)
```

```python
import functools

import jax
import jax.numpy as jnp
from jax import lax
from jax.experimental import pallas as pl
from jax.experimental.pallas import tpu as pltpu
from jax.sharding import PartitionSpec as P

DEV_GROUP = 8
GROUP = 1
MESH = pl.DeviceIdType.MESH
F32 = jnp.float32
BF16 = jnp.bfloat16


def nn(a, b):
    return lax.dot_general(a, b, (((1,), (0,)), ((), ())), preferred_element_type=F32)


def nt(a, b):
    return lax.dot_general(a, b, (((1,), (1,)), ((), ())), preferred_element_type=F32)


def split(a):
    high = a.astype(BF16)
    return high, (a - high.astype(F32)).astype(BF16)


def three(dot, a, b):
    return dot(a[0], b[0]) + (dot(a[0], b[1]) + dot(a[1], b[0]))


def iota(shape, dim):
    return lax.broadcasted_iota(jnp.int32, shape, dim)


def kernel(
    peers, slices, groups, *refs
):
    sources, refs = refs[:14], refs[14:]
    gx_ref, gbc_ref, gdt_ref, fin = refs[:4]
    inputs, refs = refs[4:18], refs[18:]
    owner, lens, bias, a_log, skip, x_ref, bc_ref, dt_ref, cot_ref = inputs[:9]
    ssm_ref, cx_ref, cbc_ref, wx_ref, wbc_ref = inputs[9:]
    (
    msg, state, gath, msg_out, state_out, pad_x, pad_bc, dpx, dpbc, dw_ref, taps, raw, back,
    sem_in, sem_msg, sem_state, sem_gath, sem_taps, sem_back, sem_fin,
    ) = refs
    mine = lax.axis_index("exch")
    me = lax.axis_index("dp")
    depth, prompts, channels = cx_ref.shape
    taps_n = depth + 1
    responses = lens.shape[0]
    heads = bias.shape[0]
    width = channels // heads
    tokens = x_ref.shape[0]
    length = tokens // responses
    rows = bc_ref.shape[0]
    pair = cbc_ref.shape[2]
    half = pair // 2
    lanes = responses * heads
    base = 8 - depth

    def along(offset):
        return {"exch": lax.rem(mine + offset, peers)}

    def across(offset):
        return {"dp": lax.rem(me + offset, slices)}

    barrier = pltpu.get_barrier_semaphore()
    for offset in range(1, slices):
        pl.semaphore_signal(barrier, inc=1, device_id=across(offset), device_id_type=MESH)
    for offset in range(1, peers):
        pl.semaphore_signal(barrier, inc=1, device_id=along(offset), device_id_type=MESH)

    loads = [
        pltpu.make_async_copy(src, dst, sem_in.at[i])
        for i, (src, dst) in enumerate(zip(sources, inputs))
    ]
    sooner = (0, 10, 11, 9, 6)
    later = [i for i in range(len(loads)) if i not in sooner]
    for i in sooner:
        loads[i].start()
    for i in later:
        loads[i].start()
    for i in sooner:
        loads[i].wait()

    tails = [
        jnp.concatenate([cx_ref[k].astype(F32), cbc_ref[k].astype(F32)], axis=1)
        for k in range(depth)
    ]

    def fill(target, msg_dst, state_dst):
        small = [jnp.zeros((1, channels + pair), F32)] * depth
        flag = jnp.zeros((1, channels + pair), F32)
        big = jnp.zeros(ssm_ref.shape[1:], F32)
        for p in range(prompts):
            weight = (owner[p] == target).astype(F32)
            for k in range(depth):
                small[k] = small[k] + tails[k][p : p + 1] * weight
            flag = flag + weight
            big = big + ssm_ref[p].astype(F32) * weight
        for k in range(depth):
            msg_dst[k : k + 1] = small[k]
        msg_dst[depth : depth + 1] = flag
        state_dst[...] = big.astype(BF16)

    for offset in range(1, peers):
        fill(lax.rem(mine + offset, peers), msg_out.at[offset], state_out.at[offset])
    fill(mine, msg.at[mine], state.at[mine])

    pl.semaphore_wait(barrier, slices - 1 + peers - 1)

    def remote(src, dst, sem, offset, where):
        copy = pltpu.make_async_remote_copy(
            src_ref=src,
            dst_ref=dst,
            send_sem=sem.at[0, offset],
            recv_sem=sem.at[1, offset],
            device_id=where,
            device_id_type=MESH,
        )
        copy.start()
        return copy

    def group_columns(ref, who):
        if groups == 1:
            return ref
        start = pl.multiple_of((who // DEV_GROUP) * pair, pair)
        return ref.at[:, pl.ds(start, pair)]

    msg_copies = [
        remote(msg_out.at[o], msg.at[mine], sem_msg, o, along(o)) for o in range(1, peers)
    ]
    gath_copies = [
        remote(
            group_columns(bc_ref, lax.rem(me + o, slices)),
            gath.at[me],
            sem_gath,
            o,
            across(o),
        )
        for o in range(1, slices)
    ]
    state_copies = [
        remote(state_out.at[o], state.at[mine], sem_state, o, along(o))
        for o in range(peers - 1, 0, -1)
    ]
    gath[me] = group_columns(bc_ref, me)[...]

    for i in later:
        loads[i].wait()

    row_head = lax.rem(iota((lanes, 1), 0), heads)

    def per_row(ref):
        out = jnp.zeros((lanes, 1), F32)
        for h in range(heads):
            out = jnp.where(row_head == h, ref[h], out)
        return out

    lane_head = iota((1, channels), 1) // width
    skip_row = jnp.zeros((1, channels), F32)
    for h in range(heads):
        skip_row = jnp.where(lane_head == h, skip[h], skip_row)
    dt_in = jnp.concatenate(
        [dt_ref[:, r * length : (r + 1) * length].astype(F32) for r in range(responses)], axis=0
    )
    dt_pre = dt_in + per_row(bias)
    small = jnp.exp(-jnp.abs(dt_pre))
    above = 1.0 + small
    log1p = jnp.where(above == 1.0, small, jnp.log(above) * (small / (above - 1.0)))
    dt = jnp.maximum(dt_pre, 0.0) + log1p
    rate = jnp.exp(per_row(a_log))
    first = iota((length, length), 0)
    second = iota((length, length), 1)
    upto = (first <= second).astype(F32)
    onward = (first >= second).astype(F32)
    causal = first <= second
    logs = lax.dot_general(
        -rate * dt,
        upto,
        (((1,), (0,)), ((), ())),
        preferred_element_type=F32,
        precision=lax.Precision.HIGHEST,
    )
    entry = jnp.exp(logs)
    logs_col = logs.T
    dt_col = dt.T
    entry_col = entry.T

    def spread_heads(cols, r):
        parts = [
            jnp.broadcast_to(cols[:, r * heads + h : r * heads + h + 1], (length, width))
            for h in range(heads)
        ]
        return jnp.concatenate(parts, axis=1)

    def indicator(r):
        row = iota((lanes, channels), 0)
        head = iota((lanes, channels), 1) // width
        return (row == r * heads + head).astype(BF16)

    for r in range(responses):
        block = slice(r * length, (r + 1) * length)
        pad_x[r, 8 : 8 + length] = x_ref[block].astype(F32)
    cots = []
    for r in range(responses):
        block = slice(r * length, (r + 1) * length)
        live = iota((length, 1), 0) < lens[r]
        cots.append(jnp.where(live, cot_ref[block].astype(F32), 0.0))

    for copy in msg_copies:
        copy.wait_recv()
    weights = [[None] * peers for _ in range(prompts)]
    seen = jnp.zeros((1, channels + pair), F32)
    for z in range(peers):
        present = msg[z, depth : depth + 1]
        for j in range(prompts):
            weights[j][z] = jnp.where(seen == float(j), present, 0.0)
        seen = seen + present
    for r in range(responses):
        prev = jnp.zeros((depth, channels + pair), F32)
        for z in range(peers):
            prev = prev + msg[z, 0:depth] * weights[r // GROUP][z]
        pad_x[r, base:8] = prev[:, :channels]
        pad_bc[r, base:8] = prev[:, channels:]

    def convolve(pad, weight, r):
        pre = pad[r, base : base + length] * weight[0:1]
        for k in range(1, taps_n):
            pre = pre + pad[r, base + k : base + k + length] * weight[k : k + 1]
        gate = 1.0 / (1.0 + jnp.exp(-pre))
        return pre * gate, gate * (1.0 + pre * (1.0 - gate))

    wx = wx_ref[...]
    wbc = wbc_ref[...]
    x_acts = [convolve(pad_x, wx, r) for r in range(responses)]

    for copy in gath_copies:
        copy.wait_recv()
    slots = length // rows
    for d in range(slices):
        r, place = d // slots, d % slots
        pad_bc[r, 8 + place * rows : 8 + (place + 1) * rows] = gath[d].astype(F32)
    bc_acts = [convolve(pad_bc, wbc, r) for r in range(responses)]

    across_rows = jnp.zeros((lanes, length), F32)
    dt_first = jnp.zeros((lanes, length), F32)
    row_index = iota((lanes, 1), 0)
    skip_sum = jnp.zeros((1, channels), F32)
    grad_wx = jnp.zeros((taps_n, channels), F32)
    b_grads, c_grads = [], []

    def weight_grad(grad, pad, r):
        parts = [
            jnp.sum(grad * pad[r, base + k : base + k + length], axis=0, keepdims=True)
            for k in range(taps_n)
        ]
        return jnp.concatenate(parts, axis=0)

    def input_grad(ref, weight, r):
        total = ref[r, depth : depth + length] * weight[0:1]
        for k in range(1, taps_n):
            total = total + ref[r, depth - k : depth - k + length] * weight[k : k + 1]
        return total

    for r in range(responses):
        act, slope = x_acts[r]
        cot = cots[r]
        cot_b = cot.astype(BF16)
        dt_full = spread_heads(dt_col, r)
        weighted = split(act * dt_full)
        proj_b = split(bc_acts[r][0][:, :half])
        proj_c = split(bc_acts[r][0][:, half:])
        scores = three(nt, proj_b, proj_c)
        score_grad = jnp.zeros((length, length), F32)
        for h in range(heads):
            i = r * heads + h
            cols = slice(h * width, (h + 1) * width)
            cot_h = cot_b[:, cols]
            gap = logs[i : i + 1] - logs_col[:, i : i + 1]
            decay = jnp.where(causal, jnp.exp(jnp.where(causal, gap, 0.0)), 0.0)
            mix = scores * decay
            mix_grad = nt(weighted[0][:, cols], cot_h) + nt(weighted[1][:, cols], cot_h)
            high, low = split(mix)
            dw_ref[r, :, cols] = nn(high, cot_h) + nn(low, cot_h)
            score_grad = score_grad + mix_grad * decay
            found = jnp.sum(mix_grad * mix, axis=0, keepdims=True)
            across_rows = jnp.where(row_index == i, found, across_rows)
        dw = dw_ref[r]
        prod = split(dw * act)
        mark = indicator(r)
        dt_first = dt_first + (nt(mark, prod[0]) + nt(mark, prod[1]))
        skip_sum = skip_sum + jnp.sum(cot * act, axis=0, keepdims=True)
        pre_grad = (dw * dt_full + skip_row * cot) * slope
        dpx[r, 0:length] = pre_grad
        dpx[r, length : length + 8] = jnp.zeros((8, channels), F32)
        grad_wx = grad_wx + weight_grad(pre_grad, pad_x, r)
        gx_ref[r * length : (r + 1) * length] = input_grad(dpx, wx, r).astype(BF16)
        b_grads.append(three(nn, split(score_grad), proj_c))
        c_grads.append(three(nn, split(score_grad.T), proj_b))

    for copy in state_copies:
        copy.wait_recv()
    starts = []
    grad_taps = jnp.zeros((taps_n, pair), F32)
    for r in range(responses):
        start = jnp.zeros(state.shape[1:], F32)
        for z in range(peers):
            pick = weights[r // GROUP][z][:, : state.shape[2]]
            start = start + state[z].astype(F32) * pick
        start = start.astype(BF16)
        starts.append(start)
        fed = split(cots[r] * spread_heads(entry_col, r))
        c_grad = c_grads[r] + (nn(fed[0], start) + nn(fed[1], start))
        slope = bc_acts[r][1]
        pre_grad = jnp.concatenate([b_grads[r], c_grad], axis=1) * slope
        dpbc[r, 0:length] = pre_grad
        dpbc[r, length : length + 8] = jnp.zeros((8, pair), F32)
        grad_taps = grad_taps + weight_grad(pre_grad, pad_bc, r)

    taps[me, 0:taps_n] = grad_taps
    taps_copies = [
        remote(taps.at[me], taps.at[me], sem_taps, o, across(o)) for o in range(1, slices)
    ]
    for r in range(responses):
        block = input_grad(dpbc, wbc, r)
        for place in range(slots):
            raw[r * slots + place] = block[place * rows : (place + 1) * rows]
    back_copies = [
        remote(raw.at[lax.rem(me + o, slices)], back.at[me], sem_back, o, across(o))
        for o in range(1, slices)
    ]
    back[me] = raw[me]

    entry_grad = jnp.zeros((lanes, length), F32)
    for r in range(responses):
        proj_c = split(bc_acts[r][0][:, half:])
        carried = nt(proj_c[0], starts[r]) + nt(proj_c[1], starts[r])
        prod = split(carried * cots[r])
        mark = indicator(r)
        entry_grad = entry_grad + (nt(mark, prod[0]) + nt(mark, prod[1]))
    log_grad = across_rows + entry * entry_grad - dt * dt_first
    step_grad = lax.dot_general(
        log_grad,
        onward,
        (((1,), (0,)), ((), ())),
        preferred_element_type=F32,
        precision=lax.Precision.HIGHEST,
    )
    dt_grad = dt_first - rate * step_grad
    raw_grad = dt_grad * (1.0 / (1.0 + jnp.exp(-dt_pre)))
    for r in range(responses):
        gdt_ref[:, r * length : (r + 1) * length] = raw_grad[
            r * heads : (r + 1) * heads
        ].astype(BF16)
    bias_rows = jnp.sum(raw_grad, axis=1, keepdims=True)
    decay_rows = -rate * jnp.sum(dt * step_grad, axis=1, keepdims=True)
    bias_grad = jnp.zeros((heads, 1), F32)
    decay_grad = jnp.zeros((heads, 1), F32)
    for r in range(responses):
        bias_grad = bias_grad + bias_rows[r * heads : (r + 1) * heads]
        decay_grad = decay_grad + decay_rows[r * heads : (r + 1) * heads]
    own = iota((heads, channels), 0) == iota((heads, channels), 1) // width
    skip_grad = jnp.sum(jnp.where(own, skip_sum, 0.0), axis=1, keepdims=True)
    column = iota((heads, half), 1)
    head_block = jnp.where(
        column == 0,
        bias_grad,
        jnp.where(column == 1, decay_grad, jnp.where(column == 2, skip_grad, 0.0)),
    )
    fin[mine] = jnp.zeros(fin.shape[1:], F32)
    fin[mine, 0:taps_n, 0:channels] = grad_wx
    fin[mine, 8 : 8 + heads, 0:half] = head_block

    for copy in taps_copies:
        copy.wait_recv()
    for q in range(groups):
        total = taps[q * DEV_GROUP, 0:taps_n]
        for d in range(1, DEV_GROUP):
            total = total + taps[q * DEV_GROUP + d, 0:taps_n]
        fin[mine, 16 : 16 + taps_n, q * pair : (q + 1) * pair] = total
    fin_copies = [
        remote(fin.at[mine], fin.at[mine], sem_fin, o, along(o)) for o in range(1, peers)
    ]

    for copy in back_copies:
        copy.wait_recv()
    for q in range(groups):
        total = back[q * DEV_GROUP]
        for d in range(1, DEV_GROUP):
            total = total + back[q * DEV_GROUP + d]
        gbc_ref[:, q * pair : (q + 1) * pair] = total.astype(BF16)

    for copy in fin_copies:
        copy.wait_recv()
    for copy in msg_copies + gath_copies + state_copies + taps_copies + back_copies + fin_copies:
        copy.wait_send()


def finish(
    gx_in, gbc_in, gdt_in, fin, gx_ref, gbc_ref, gdt_ref, gwx_ref, gtaps_ref, gheads_ref, sems
):
    copies = [
        pltpu.make_async_copy(src, dst, sems.at[i])
        for i, (src, dst) in enumerate(
            ((gx_in, gx_ref), (gbc_in, gbc_ref), (gdt_in, gdt_ref))
        )
    ]
    for copy in copies:
        copy.start()
    taps_n, channels = gwx_ref.shape
    heads = gheads_ref.shape[1]
    pairs = gtaps_ref.shape[1]
    total = fin[0]
    for z in range(1, fin.shape[0]):
        total = total + fin[z]
    gwx_ref[...] = total[0:taps_n, 0:channels]
    gtaps_ref[...] = total[16 : 16 + taps_n, 0:pairs]
    gheads_ref[...] = total[8:16, 0:128].T[0:3, 0:heads]
    for copy in copies:
        copy.wait()


def local(
    x_raw, bc_raw, dt_raw, cotangent, ssm_state, conv_x_state, conv_bc_state, owner, resp_len,
    conv_x_weight, conv_bc_weight, dt_bias, a_log, skip_d,
):
    peers = lax.axis_size("exch")
    slices = lax.axis_size("dp")
    prompts, heads, width, nstate = ssm_state.shape
    channels = x_raw.shape[1]
    pair = 2 * nstate
    depth = conv_x_state.shape[1]
    responses = resp_len.shape[0]
    tokens = x_raw.shape[0]
    length = tokens // responses
    rows, all_pairs = bc_raw.shape
    groups = all_pairs // pair
    bc_state, bc_weight = conv_bc_state, conv_bc_weight
    if groups > 1:
        first = (lax.axis_index("dp") // DEV_GROUP) * pair
        bc_state = lax.dynamic_slice_in_dim(conv_bc_state, first, pair, 2)
        bc_weight = lax.dynamic_slice_in_dim(conv_bc_weight, first, pair, 1)
    ssm = ssm_state.reshape(prompts, heads * width, nstate)
    wide = max(all_pairs, channels)
    vmem = pl.BlockSpec(memory_space=pltpu.VMEM)
    dma = pltpu.SemaphoreType.DMA
    outs = (
        jax.ShapeDtypeStruct((tokens, channels), BF16),
        jax.ShapeDtypeStruct((rows, all_pairs), BF16),
        jax.ShapeDtypeStruct((heads, tokens), BF16),
        jax.ShapeDtypeStruct((depth + 1, channels), F32),
        jax.ShapeDtypeStruct((depth + 1, all_pairs), F32),
        jax.ShapeDtypeStruct((3, heads), F32),
    )
    staged = tuple(pltpu.VMEM(out.shape, out.dtype) for out in outs[:3])
    staged = staged + (pltpu.VMEM((peers, 24, wide), F32),)
    args = (
        owner, resp_len, dt_bias, a_log, skip_d, x_raw, bc_raw, dt_raw, cotangent, ssm,
        conv_x_state.transpose(1, 0, 2), bc_state.transpose(1, 0, 2), conv_x_weight, bc_weight,
    )
    held = pl.pallas_call(
        functools.partial(kernel, peers, slices, groups),
        out_shape=staged,
        in_specs=[pl.BlockSpec(memory_space=pltpu.HBM)] * 14,
        out_specs=[vmem] * 4,
        scratch_shapes=[pltpu.SMEM(a.shape, a.dtype) for a in args[:5]]
        + [pltpu.VMEM(a.shape, a.dtype) for a in args[5:]]
        + [
            pltpu.VMEM((peers, 8, channels + pair), F32),
            pltpu.VMEM((peers, heads * width, nstate), BF16),
            pltpu.VMEM((slices, rows, pair), BF16),
            pltpu.VMEM((peers, 8, channels + pair), F32),
            pltpu.VMEM((peers, heads * width, nstate), BF16),
            pltpu.VMEM((responses, length + 8, channels), F32),
            pltpu.VMEM((responses, length + 8, pair), F32),
            pltpu.VMEM((responses, length + 8, channels), F32),
            pltpu.VMEM((responses, length + 8, pair), F32),
            pltpu.VMEM((responses, length, channels), F32),
            pltpu.VMEM((slices, 8, pair), F32),
            pltpu.VMEM((slices, rows, pair), F32),
            pltpu.VMEM((slices, rows, pair), F32),
            dma((14,)),
            dma((2, peers)),
            dma((2, peers)),
            dma((2, slices)),
            dma((2, slices)),
            dma((2, slices)),
            dma((2, peers)),
        ],
        compiler_params=pltpu.CompilerParams(
            collective_id=0, has_side_effects=True
        ),
    )(*args)
    anywhere = pl.BlockSpec(memory_space=pl.ANY)
    return pl.pallas_call(
        finish,
        out_shape=outs,
        in_specs=[vmem] * 4,
        out_specs=[anywhere] * 3 + [vmem] * 3,
        scratch_shapes=[dma((3,))],
        compiler_params=pltpu.CompilerParams(vmem_limit_bytes=16 * 1024 * 1024),
    )(*held)


def solution(mesh):
    in_specs = (
        P("exch", "dp"),
        P(("exch", "dp"), None),
        P("dp", "exch"),
        P("exch", "dp"),
        P("exch", "dp", None, None),
        P("exch", None, "dp"),
        P("exch", None, None),
        P("exch"),
        P("exch"),
        P(None, "dp"),
        P(),
        P("dp"),
        P("dp"),
        P("dp"),
    )
    out_specs = (
        P("exch", "dp"),
        P(("exch", "dp"), None),
        P("dp", "exch"),
        P(None, "dp"),
        P(),
        P(None, "dp"),
    )
    return jax.shard_map(local, mesh=mesh, in_specs=in_specs, out_specs=out_specs, check_vma=False)
```

```python
import functools

import jax
import jax.numpy as jnp
from jax import lax
from jax.experimental import pallas as pl
from jax.experimental.pallas import tpu as pltpu
from jax.sharding import PartitionSpec as P

DEV_GROUP = 8
GROUP = 1
MESH = pl.DeviceIdType.MESH
F32 = jnp.float32
BF16 = jnp.bfloat16


def nn(a, b):
    return lax.dot_general(a, b, (((1,), (0,)), ((), ())), preferred_element_type=F32)


def nt(a, b):
    return lax.dot_general(a, b, (((1,), (1,)), ((), ())), preferred_element_type=F32)


def split(a):
    high = a.astype(BF16)
    return high, (a - high.astype(F32)).astype(BF16)


def three(dot, a, b):
    return dot(a[0], b[0]) + (dot(a[0], b[1]) + dot(a[1], b[0]))


def iota(shape, dim):
    return lax.broadcasted_iota(jnp.int32, shape, dim)


def kernel(
    peers, slices, groups, *refs
):
    sources, refs = refs[:14], refs[14:]
    gx_ref, gbc_ref, gdt_ref, fin = refs[:4]
    inputs, refs = refs[4:18], refs[18:]
    owner, lens, bias, a_log, skip, x_ref, bc_ref, dt_ref, cot_ref = inputs[:9]
    ssm_ref, cx_ref, cbc_ref, wx_ref, wbc_ref = inputs[9:]
    (
    msg, state, gath, msg_out, state_out, pad_x, pad_bc, dpx, dpbc, dw_ref, taps, raw, back,
    sem_in, sem_msg, sem_state, sem_gath, sem_taps, sem_back, sem_wx, sem_heads, sem_fin,
    ) = refs
    mine = lax.axis_index("exch")
    me = lax.axis_index("dp")
    depth, prompts, channels = cx_ref.shape
    taps_n = depth + 1
    responses = lens.shape[0]
    heads = bias.shape[0]
    width = channels // heads
    tokens = x_ref.shape[0]
    length = tokens // responses
    rows = bc_ref.shape[0]
    pair = cbc_ref.shape[2]
    half = pair // 2
    lanes = responses * heads
    base = 8 - depth

    def along(offset):
        return {"exch": lax.rem(mine + offset, peers)}

    def across(offset):
        return {"dp": lax.rem(me + offset, slices)}

    barrier = pltpu.get_barrier_semaphore()
    for offset in range(1, slices):
        pl.semaphore_signal(barrier, inc=1, device_id=across(offset), device_id_type=MESH)
    for offset in range(1, peers):
        pl.semaphore_signal(barrier, inc=1, device_id=along(offset), device_id_type=MESH)

    loads = [
        pltpu.make_async_copy(src, dst, sem_in.at[i])
        for i, (src, dst) in enumerate(zip(sources, inputs))
    ]
    sooner = (0, 10, 11, 9, 6)
    later = [i for i in range(len(loads)) if i not in sooner]
    for i in sooner:
        loads[i].start()
    for i in later:
        loads[i].start()
    for i in sooner:
        loads[i].wait()

    tails = [
        jnp.concatenate([cx_ref[k].astype(F32), cbc_ref[k].astype(F32)], axis=1)
        for k in range(depth)
    ]

    def fill(target, msg_dst, state_dst):
        small = [jnp.zeros((1, channels + pair), F32)] * depth
        flag = jnp.zeros((1, channels + pair), F32)
        big = jnp.zeros(ssm_ref.shape[1:], F32)
        for p in range(prompts):
            weight = (owner[p] == target).astype(F32)
            for k in range(depth):
                small[k] = small[k] + tails[k][p : p + 1] * weight
            flag = flag + weight
            big = big + ssm_ref[p].astype(F32) * weight
        msg_dst[...] = jnp.concatenate(small + [flag], axis=0).astype(BF16)
        state_dst[...] = big.astype(BF16)

    for offset in range(1, peers):
        fill(lax.rem(mine + offset, peers), msg_out.at[offset], state_out.at[offset])
    fill(mine, msg.at[mine], state.at[mine])

    pl.semaphore_wait(barrier, slices - 1 + peers - 1)

    def remote(src, dst, sem, offset, where):
        copy = pltpu.make_async_remote_copy(
            src_ref=src,
            dst_ref=dst,
            send_sem=sem.at[0, offset],
            recv_sem=sem.at[1, offset],
            device_id=where,
            device_id_type=MESH,
        )
        copy.start()
        return copy

    def group_columns(ref, who):
        if groups == 1:
            return ref
        start = pl.multiple_of((who // DEV_GROUP) * pair, pair)
        return ref.at[:, pl.ds(start, pair)]

    msg_copies = [
        remote(msg_out.at[o], msg.at[mine], sem_msg, o, along(o)) for o in range(1, peers)
    ]
    gath_copies = [
        remote(
            group_columns(bc_ref, lax.rem(me + o, slices)),
            gath.at[me],
            sem_gath,
            o,
            across(o),
        )
        for o in range(1, slices)
    ]
    state_copies = [
        remote(state_out.at[o], state.at[mine], sem_state, o, along(o))
        for o in range(peers - 1, 0, -1)
    ]
    gath[me] = group_columns(bc_ref, me)[...]

    for i in later:
        loads[i].wait()

    row_head = lax.rem(iota((lanes, 1), 0), heads)

    def per_row(ref):
        out = jnp.zeros((lanes, 1), F32)
        for h in range(heads):
            out = jnp.where(row_head == h, ref[h], out)
        return out

    lane_head = iota((1, channels), 1) // width
    skip_row = jnp.zeros((1, channels), F32)
    for h in range(heads):
        skip_row = jnp.where(lane_head == h, skip[h], skip_row)
    dt_in = jnp.concatenate(
        [dt_ref[:, r * length : (r + 1) * length].astype(F32) for r in range(responses)], axis=0
    )
    dt_pre = dt_in + per_row(bias)
    small = jnp.exp(-jnp.abs(dt_pre))
    above = 1.0 + small
    log1p = jnp.where(above == 1.0, small, jnp.log(above) * (small / (above - 1.0)))
    dt = jnp.maximum(dt_pre, 0.0) + log1p
    rate = jnp.exp(per_row(a_log))
    first = iota((length, length), 0)
    second = iota((length, length), 1)
    upto = (first <= second).astype(F32)
    onward = (first >= second).astype(F32)
    causal = first <= second
    logs = lax.dot_general(
        -rate * dt,
        upto,
        (((1,), (0,)), ((), ())),
        preferred_element_type=F32,
        precision=lax.Precision.HIGHEST,
    )
    entry = jnp.exp(logs)
    logs_col = logs.T
    dt_col = dt.T
    entry_col = entry.T

    def spread_heads(cols, r):
        parts = [
            jnp.broadcast_to(cols[:, r * heads + h : r * heads + h + 1], (length, width))
            for h in range(heads)
        ]
        return jnp.concatenate(parts, axis=1)

    def indicator(r):
        row = iota((lanes, channels), 0)
        head = iota((lanes, channels), 1) // width
        return (row == r * heads + head).astype(BF16)

    for r in range(responses):
        block = slice(r * length, (r + 1) * length)
        pad_x[r, 8 : 8 + length] = x_ref[block].astype(F32)
    cots = []
    for r in range(responses):
        block = slice(r * length, (r + 1) * length)
        live = iota((length, 1), 0) < lens[r]
        cots.append(jnp.where(live, cot_ref[block].astype(F32), 0.0))

    for copy in msg_copies:
        copy.wait_recv()
    got = [msg[z].astype(F32) for z in range(peers)]
    weights = [[None] * peers for _ in range(prompts)]
    seen = jnp.zeros((1, channels + pair), F32)
    for z in range(peers):
        present = got[z][depth : depth + 1]
        for j in range(prompts):
            weights[j][z] = jnp.where(seen == float(j), present, 0.0)
        seen = seen + present
    for r in range(responses):
        prev = jnp.zeros((depth, channels + pair), F32)
        for z in range(peers):
            prev = prev + got[z][0:depth] * weights[r // GROUP][z]
        pad_x[r, base:8] = prev[:, :channels]
        pad_bc[r, base:8] = prev[:, channels:]

    def convolve(pad, weight, r):
        pre = pad[r, base : base + length] * weight[0:1]
        for k in range(1, taps_n):
            pre = pre + pad[r, base + k : base + k + length] * weight[k : k + 1]
        gate = 1.0 / (1.0 + jnp.exp(-pre))
        return pre * gate, gate * (1.0 + pre * (1.0 - gate))

    wx = wx_ref[...]
    wbc = wbc_ref[...]
    x_acts = [convolve(pad_x, wx, r) for r in range(responses)]

    for copy in gath_copies:
        copy.wait_recv()
    slots = length // rows
    for d in range(slices):
        r, place = d // slots, d % slots
        pad_bc[r, 8 + place * rows : 8 + (place + 1) * rows] = gath[d].astype(F32)
    bc_acts = [convolve(pad_bc, wbc, r) for r in range(responses)]

    across_rows = jnp.zeros((lanes, length), F32)
    dt_first = jnp.zeros((lanes, length), F32)
    row_index = iota((lanes, 1), 0)
    skip_sum = jnp.zeros((1, channels), F32)
    grad_wx = jnp.zeros((taps_n, channels), F32)
    b_grads, c_grads = [], []

    def weight_grad(grad, pad, r):
        parts = [
            jnp.sum(grad * pad[r, base + k : base + k + length], axis=0, keepdims=True)
            for k in range(taps_n)
        ]
        return jnp.concatenate(parts, axis=0)

    def input_grad(ref, weight, r):
        total = ref[r, depth : depth + length] * weight[0:1]
        for k in range(1, taps_n):
            total = total + ref[r, depth - k : depth - k + length] * weight[k : k + 1]
        return total

    for r in range(responses):
        act, slope = x_acts[r]
        cot = cots[r]
        cot_b = cot.astype(BF16)
        dt_full = spread_heads(dt_col, r)
        weighted = split(act * dt_full)
        proj_b = split(bc_acts[r][0][:, :half])
        proj_c = split(bc_acts[r][0][:, half:])
        scores = three(nt, proj_b, proj_c)
        score_grad = jnp.zeros((length, length), F32)
        for h in range(heads):
            i = r * heads + h
            cols = slice(h * width, (h + 1) * width)
            cot_h = cot_b[:, cols]
            gap = logs[i : i + 1] - logs_col[:, i : i + 1]
            decay = jnp.where(causal, jnp.exp(jnp.where(causal, gap, 0.0)), 0.0)
            mix = scores * decay
            mix_grad = nt(weighted[0][:, cols], cot_h) + nt(weighted[1][:, cols], cot_h)
            high, low = split(mix)
            dw_ref[r, :, cols] = nn(high, cot_h) + nn(low, cot_h)
            score_grad = score_grad + mix_grad * decay
            found = jnp.sum(mix_grad * mix, axis=0, keepdims=True)
            across_rows = jnp.where(row_index == i, found, across_rows)
        dw = dw_ref[r]
        prod = split(dw * act)
        mark = indicator(r)
        dt_first = dt_first + (nt(mark, prod[0]) + nt(mark, prod[1]))
        skip_sum = skip_sum + jnp.sum(cot * act, axis=0, keepdims=True)
        pre_grad = (dw * dt_full + skip_row * cot) * slope
        dpx[r, 0:length] = pre_grad
        dpx[r, length : length + 8] = jnp.zeros((8, channels), F32)
        grad_wx = grad_wx + weight_grad(pre_grad, pad_x, r)
        gx_ref[r * length : (r + 1) * length] = input_grad(dpx, wx, r).astype(BF16)
        b_grads.append(three(nn, split(score_grad), proj_c))
        c_grads.append(three(nn, split(score_grad.T), proj_b))

    def send_rows(row, sem):
        part = fin.at[mine, pl.ds(row, 8)]
        return [remote(part, part, sem, o, along(o)) for o in range(1, peers)]

    fin[mine] = jnp.zeros(fin.shape[1:], F32)
    fin[mine, 0:taps_n, 0:channels] = grad_wx
    fin_copies = send_rows(0, sem_wx)

    for copy in state_copies:
        copy.wait_recv()
    starts = []
    grad_taps = jnp.zeros((taps_n, pair), F32)
    for r in range(responses):
        start = jnp.zeros(state.shape[1:], F32)
        for z in range(peers):
            pick = weights[r // GROUP][z][:, : state.shape[2]]
            start = start + state[z].astype(F32) * pick
        start = start.astype(BF16)
        starts.append(start)
        fed = split(cots[r] * spread_heads(entry_col, r))
        c_grad = c_grads[r] + (nn(fed[0], start) + nn(fed[1], start))
        slope = bc_acts[r][1]
        pre_grad = jnp.concatenate([b_grads[r], c_grad], axis=1) * slope
        dpbc[r, 0:length] = pre_grad
        dpbc[r, length : length + 8] = jnp.zeros((8, pair), F32)
        grad_taps = grad_taps + weight_grad(pre_grad, pad_bc, r)

    taps[me, 0:taps_n] = grad_taps
    taps_copies = [
        remote(taps.at[me], taps.at[me], sem_taps, o, across(o)) for o in range(1, slices)
    ]
    for r in range(responses):
        block = input_grad(dpbc, wbc, r)
        for place in range(slots):
            raw[r * slots + place] = block[place * rows : (place + 1) * rows]
    back_copies = [
        remote(raw.at[lax.rem(me + o, slices)], back.at[me], sem_back, o, across(o))
        for o in range(1, slices)
    ]
    back[me] = raw[me]

    entry_grad = jnp.zeros((lanes, length), F32)
    for r in range(responses):
        proj_c = split(bc_acts[r][0][:, half:])
        carried = nt(proj_c[0], starts[r]) + nt(proj_c[1], starts[r])
        prod = split(carried * cots[r])
        mark = indicator(r)
        entry_grad = entry_grad + (nt(mark, prod[0]) + nt(mark, prod[1]))
    log_grad = across_rows + entry * entry_grad - dt * dt_first
    step_grad = lax.dot_general(
        log_grad,
        onward,
        (((1,), (0,)), ((), ())),
        preferred_element_type=F32,
        precision=lax.Precision.HIGHEST,
    )
    dt_grad = dt_first - rate * step_grad
    raw_grad = dt_grad * (1.0 / (1.0 + jnp.exp(-dt_pre)))
    for r in range(responses):
        gdt_ref[:, r * length : (r + 1) * length] = raw_grad[
            r * heads : (r + 1) * heads
        ].astype(BF16)
    bias_rows = jnp.sum(raw_grad, axis=1, keepdims=True)
    decay_rows = -rate * jnp.sum(dt * step_grad, axis=1, keepdims=True)
    bias_grad = jnp.zeros((heads, 1), F32)
    decay_grad = jnp.zeros((heads, 1), F32)
    for r in range(responses):
        bias_grad = bias_grad + bias_rows[r * heads : (r + 1) * heads]
        decay_grad = decay_grad + decay_rows[r * heads : (r + 1) * heads]
    own = iota((heads, channels), 0) == iota((heads, channels), 1) // width
    skip_grad = jnp.sum(jnp.where(own, skip_sum, 0.0), axis=1, keepdims=True)
    column = iota((heads, half), 1)
    head_block = jnp.where(
        column == 0,
        bias_grad,
        jnp.where(column == 1, decay_grad, jnp.where(column == 2, skip_grad, 0.0)),
    )
    fin[mine, 8 : 8 + heads, 0:half] = head_block
    fin_copies = fin_copies + send_rows(8, sem_heads)

    for copy in taps_copies:
        copy.wait_recv()
    for q in range(groups):
        total = taps[q * DEV_GROUP, 0:taps_n]
        for d in range(1, DEV_GROUP):
            total = total + taps[q * DEV_GROUP + d, 0:taps_n]
        fin[mine, 16 : 16 + taps_n, q * pair : (q + 1) * pair] = total
    fin_copies = fin_copies + send_rows(16, sem_fin)

    for copy in back_copies:
        copy.wait_recv()
    for q in range(groups):
        total = back[q * DEV_GROUP]
        for d in range(1, DEV_GROUP):
            total = total + back[q * DEV_GROUP + d]
        gbc_ref[:, q * pair : (q + 1) * pair] = total.astype(BF16)

    for copy in fin_copies:
        copy.wait_recv()
    for copy in msg_copies + gath_copies + state_copies + taps_copies + back_copies + fin_copies:
        copy.wait_send()


def finish(
    gx_in, gbc_in, gdt_in, fin, gx_ref, gbc_ref, gdt_ref, gwx_ref, gtaps_ref, gheads_ref, sems
):
    copies = [
        pltpu.make_async_copy(src, dst, sems.at[i])
        for i, (src, dst) in enumerate(
            ((gx_in, gx_ref), (gbc_in, gbc_ref), (gdt_in, gdt_ref))
        )
    ]
    for copy in copies:
        copy.start()
    taps_n, channels = gwx_ref.shape
    heads = gheads_ref.shape[1]
    pairs = gtaps_ref.shape[1]
    total = fin[0]
    for z in range(1, fin.shape[0]):
        total = total + fin[z]
    gwx_ref[...] = total[0:taps_n, 0:channels]
    gtaps_ref[...] = total[16 : 16 + taps_n, 0:pairs]
    gheads_ref[...] = total[8:16, 0:128].T[0:3, 0:heads]
    for copy in copies:
        copy.wait()


def local(
    x_raw, bc_raw, dt_raw, cotangent, ssm_state, conv_x_state, conv_bc_state, owner, resp_len,
    conv_x_weight, conv_bc_weight, dt_bias, a_log, skip_d,
):
    peers = lax.axis_size("exch")
    slices = lax.axis_size("dp")
    prompts, heads, width, nstate = ssm_state.shape
    channels = x_raw.shape[1]
    pair = 2 * nstate
    depth = conv_x_state.shape[1]
    responses = resp_len.shape[0]
    tokens = x_raw.shape[0]
    length = tokens // responses
    rows, all_pairs = bc_raw.shape
    groups = all_pairs // pair
    bc_state, bc_weight = conv_bc_state, conv_bc_weight
    if groups > 1:
        first = (lax.axis_index("dp") // DEV_GROUP) * pair
        bc_state = lax.dynamic_slice_in_dim(conv_bc_state, first, pair, 2)
        bc_weight = lax.dynamic_slice_in_dim(conv_bc_weight, first, pair, 1)
    ssm = ssm_state.reshape(prompts, heads * width, nstate)
    wide = max(all_pairs, channels)
    vmem = pl.BlockSpec(memory_space=pltpu.VMEM)
    dma = pltpu.SemaphoreType.DMA
    outs = (
        jax.ShapeDtypeStruct((tokens, channels), BF16),
        jax.ShapeDtypeStruct((rows, all_pairs), BF16),
        jax.ShapeDtypeStruct((heads, tokens), BF16),
        jax.ShapeDtypeStruct((depth + 1, channels), F32),
        jax.ShapeDtypeStruct((depth + 1, all_pairs), F32),
        jax.ShapeDtypeStruct((3, heads), F32),
    )
    staged = tuple(pltpu.VMEM(out.shape, out.dtype) for out in outs[:3])
    staged = staged + (pltpu.VMEM((peers, 24, wide), F32),)
    args = (
        owner, resp_len, dt_bias, a_log, skip_d, x_raw, bc_raw, dt_raw, cotangent, ssm,
        conv_x_state.transpose(1, 0, 2), bc_state.transpose(1, 0, 2), conv_x_weight, bc_weight,
    )
    held = pl.pallas_call(
        functools.partial(kernel, peers, slices, groups),
        out_shape=staged,
        in_specs=[pl.BlockSpec(memory_space=pltpu.HBM)] * 14,
        out_specs=[vmem] * 4,
        scratch_shapes=[pltpu.SMEM(a.shape, a.dtype) for a in args[:5]]
        + [pltpu.VMEM(a.shape, a.dtype) for a in args[5:]]
        + [
            pltpu.VMEM((peers, depth + 1, channels + pair), BF16),
            pltpu.VMEM((peers, heads * width, nstate), BF16),
            pltpu.VMEM((slices, rows, pair), BF16),
            pltpu.VMEM((peers, depth + 1, channels + pair), BF16),
            pltpu.VMEM((peers, heads * width, nstate), BF16),
            pltpu.VMEM((responses, length + 8, channels), F32),
            pltpu.VMEM((responses, length + 8, pair), F32),
            pltpu.VMEM((responses, length + 8, channels), F32),
            pltpu.VMEM((responses, length + 8, pair), F32),
            pltpu.VMEM((responses, length, channels), F32),
            pltpu.VMEM((slices, 8, pair), F32),
            pltpu.VMEM((slices, rows, pair), F32),
            pltpu.VMEM((slices, rows, pair), F32),
            dma((14,)),
            dma((2, peers)),
            dma((2, peers)),
            dma((2, slices)),
            dma((2, slices)),
            dma((2, slices)),
            dma((2, peers)),
            dma((2, peers)),
            dma((2, peers)),
        ],
        compiler_params=pltpu.CompilerParams(
            collective_id=0, has_side_effects=True
        ),
    )(*args)
    anywhere = pl.BlockSpec(memory_space=pl.ANY)
    return pl.pallas_call(
        finish,
        out_shape=outs,
        in_specs=[vmem] * 4,
        out_specs=[anywhere] * 3 + [vmem] * 3,
        scratch_shapes=[dma((3,))],
        compiler_params=pltpu.CompilerParams(vmem_limit_bytes=16 * 1024 * 1024),
    )(*held)


def solution(mesh):
    in_specs = (
        P("exch", "dp"),
        P(("exch", "dp"), None),
        P("dp", "exch"),
        P("exch", "dp"),
        P("exch", "dp", None, None),
        P("exch", None, "dp"),
        P("exch", None, None),
        P("exch"),
        P("exch"),
        P(None, "dp"),
        P(),
        P("dp"),
        P("dp"),
        P("dp"),
    )
    out_specs = (
        P("exch", "dp"),
        P(("exch", "dp"), None),
        P("dp", "exch"),
        P(None, "dp"),
        P(),
        P(None, "dp"),
    )
    return jax.shard_map(local, mesh=mesh, in_specs=in_specs, out_specs=out_specs, check_vma=False)
```
